32 devices in a mesh: grp: 2 (over x), tm: 4 (over y, core), tile: 4 (over z).
Axes of the slice: x: 2, y: 2, z: 4, core: 2. Of those that a mesh axis runs over, the one named last changes fastest.
Arguments:
- frames: bfloat16 [64, 1024, 1024], P(('grp', 'tm'), 'tile'), parts along dimension 0, may hold values from -3 to 3
- inverse_taps: float32 [48], replicated, may hold values from -3 to 3
- mode_rate: float32 [1024, 1024], P(None, 'tile'), may hold values from 0.00625 to 0.2
- frame_factor: float32 [64], P(('grp', 'tm')), parts along dimension 0, may hold values from 0.5 to 1
Outputs:
- superheat: bfloat16 [64, 1024, 1024], P(('grp', 'tm'), 'tile'), parts along dimension 0
The draws below stay inside these ranges and needn't reach their ends.
There are 2 independent parts, one for each index of `grp`. The reference program is written for one: setup_inputs(seed, part) draws one part's arguments, and reference() takes and returns one part's arrays. A program takes and returns all parts, laid end to end along the dimension named above; an argument that names none is the same for every part. Nothing has to cross between parts.
All inputs are finite; a program needn't handle non-finite values.
Results may differ from the reference program's by a relative error of at most 0.0097.
Values may be sent and summed in bfloat16 or wider, within the bound.
A program may use at most 128 MiB of HBM per device.

```python
import math
import jax
import jax.numpy as jnp
from jax import lax

FRAME = 1024
TAPS = 48
SPAN_SNAPSHOTS = 32


def draw_frame_factor(key, part):
    option_selector = jax.random.fold_in(key, 11)
    level_key = jax.random.fold_in(key, 23)
    sample_bunches = jax.random.randint(option_selector, (SPAN_SNAPSHOTS,), 0, 12)
    tier_sequence = jax.random.uniform(level_key, (SPAN_SNAPSHOTS,), jnp.float32, 0.5, 0.8)
    return jnp.where(sample_bunches == 0, tier_sequence, jnp.float32(1.0)).astype(jnp.float32)


def level_of(key, dims, split, low, top_value):
    loudness, own = 1.0, jax.random.fold_in(key, 6)
    for dim, blocks in split:
        draws = jnp.exp(jax.random.uniform(jax.random.fold_in(own, dim), (blocks,), jnp.float32, low / len(split), top_value / len(split)))
        loudness = loudness * jnp.repeat(draws, dims[dim] // blocks).reshape([-1 if axis == dim else 1 for axis in range(len(dims))])
    return loudness


def scatter_about(rng, dims, scale, reach, pieces=(), kind=jnp.bfloat16):
    values = scale * jax.random.normal(rng, dims, jnp.float32)
    if pieces:
        values = values * level_of(rng, dims, pieces, -0.22, 0.18)
    return jnp.clip(values, -reach, reach).astype(kind)


def setup_inputs(seed: int = 0, part: int = 0) -> dict:
    streams_of = jax.random.split(jax.random.key(seed), 5)
    own_keys = jax.random.split(jax.random.fold_in(streams_of[4], part), 5)
    return {
        "frames": scatter_about(own_keys[0], (SPAN_SNAPSHOTS, FRAME, FRAME), 0.5, 3.0, ((0, 4), (1, 4))),
        "inverse_taps": scatter_about(streams_of[1], (TAPS,), 0.5, 3.0, (), jnp.float32),
        "mode_rate": jnp.clip(jnp.exp(math.log(0.2) - 3.465736 * jax.random.uniform(streams_of[2], (FRAME, FRAME), jnp.float32) ** level_of(streams_of[2], (FRAME, FRAME), ((1, 4),), -0.2, 0.2)), 0.00625, 0.2),
        "frame_factor": draw_frame_factor(jax.random.fold_in(jax.random.fold_in(streams_of[4], part), 71), part),
    }


def cosine_matrix(points):
    freq_idx = jnp.arange(points, dtype=jnp.int32)[:, None]
    cell_idx = jnp.arange(points, dtype=jnp.int32)[None, :]
    phase = (2 * cell_idx + 1) * freq_idx % (4 * points)
    angle = jnp.pi * phase.astype(jnp.float32) / (2.0 * points)
    values = jnp.cos(angle) * jnp.sqrt(2.0 / points)
    values = jnp.where(freq_idx == 0, values / jnp.sqrt(2.0), values)
    return values.astype(jnp.bfloat16)

def reference(frames, inverse_taps, mode_rate, frame_factor):
    frame_count = frames.shape[0]
    frame_side = frames.shape[1]
    tap_count = inverse_taps.shape[0]
    taps_b = inverse_taps.astype(jnp.bfloat16).astype(jnp.float32)
    padded = jnp.concatenate([jnp.zeros((tap_count - 1, frame_side, frame_side), jnp.bfloat16), frames], axis=0)
    wall_heat_flux = jnp.zeros((frame_count, frame_side, frame_side), jnp.float32)
    for lag_index in range(tap_count):
        start = tap_count - 1 - lag_index
        wall_heat_flux = wall_heat_flux + taps_b[lag_index] * padded[start:start + frame_count].astype(jnp.float32)
    wall_heat_flux = wall_heat_flux.astype(jnp.bfloat16)
    basis = cosine_matrix(frame_side)

    def forward(frame_now):
        column_pass = jnp.dot(frame_now, basis.T, preferred_element_type=jnp.float32).astype(jnp.bfloat16)
        return jnp.dot(basis, column_pass, preferred_element_type=jnp.float32)
    spectra = lax.map(forward, wall_heat_flux)
    retain = jnp.exp(-mode_rate)

    def advance(running, inputs):
        spectrum, factor = inputs
        running = retain * factor * running + spectrum
        return (running, running.astype(jnp.bfloat16))
    _, running_b = lax.scan(advance, jnp.zeros((frame_side, frame_side), jnp.float32), (spectra, frame_factor))

    def inverse(state_now):
        row_pass = jnp.dot(basis.T, state_now, preferred_element_type=jnp.float32).astype(jnp.bfloat16)
        return jnp.dot(row_pass, basis, preferred_element_type=jnp.float32).astype(jnp.bfloat16)
    return lax.map(inverse, running_b)
```

```python
import functools

import jax
import jax.numpy as jnp
from jax import lax
from jax.experimental import pallas as pl
from jax.experimental.pallas import tpu as pltpu
from jax.sharding import PartitionSpec as P

MESH = pl.DeviceIdType.MESH
GROUP = 16
PIECE = 64
CARRY_PIECES = 4


def cosine_values(freq_idx, cell_idx, points):
    phase = (2 * cell_idx + 1) * freq_idx % (4 * points)
    angle = jnp.pi * phase.astype(jnp.float32) / (2.0 * points)
    values = jnp.cos(angle) * jnp.sqrt(2.0 / points)
    values = jnp.where(freq_idx == 0, values / jnp.sqrt(2.0), values)
    return values.astype(jnp.bfloat16)


def dot(a, b):
    return jnp.dot(a, b, preferred_element_type=jnp.float32)


def kernel(
    x_hbm, taps, rate_hbm, factor, bt_hbm, bp_hbm, out_hbm,
    x, hist, bt, bp, retain, flux, send1, colp, acc, tk, carry, cout, dec, rb, send2, rowp, outv,
    load_sem, hist_send, hist_recv, fwd_send, fwd_recv, carry_send, carry_recv,
    inv_send, inv_recv, out_sem,
):
    span, rows, side = x.shape
    hops = hist.shape[0]
    pieces, _, depth, cols = colp.shape
    tap_count = taps.shape[0]
    tiles = side // rows
    times = lax.axis_size("tm")
    j = lax.axis_index("tm")
    z = lax.axis_index("tile")

    def partner(d):
        return lax.rem(z + d, tiles)

    def source(d):
        return lax.rem(z + tiles - d, tiles)

    loads = [
        pltpu.make_async_copy(src, dst, load_sem.at[n])
        for n, (src, dst) in enumerate(((x_hbm, x), (bt_hbm, bt), (bp_hbm, bp), (rate_hbm, retain)))
    ]
    for load in loads:
        load.start()

    barrier = pltpu.get_barrier_semaphore()
    for d in range(1, tiles):
        pl.semaphore_signal(barrier, inc=1, device_id={"tile": partner(d)}, device_id_type=MESH)

    for other in (lax.rem(j + 1, times), lax.rem(j + times - 1, times)):
        pl.semaphore_signal(barrier, inc=1, device_id={"tm": other}, device_id_type=MESH)

    pl.semaphore_wait(barrier, tiles + 1)

    def piece_rows(i):
        return pl.ds(pl.multiple_of(i * PIECE, PIECE), PIECE)

    def hist_copy(h, i):
        src = x_hbm if h == 0 else hist.at[h - 1]
        return pltpu.make_async_remote_copy(
            src_ref=src.at[:, piece_rows(i), :],
            dst_ref=hist.at[h, :, piece_rows(i), :],
            send_sem=hist_send.at[h, i],
            recv_sem=hist_recv.at[h, i],
            device_id={"tm": lax.rem(j + 1, times)},
            device_id_type=MESH,
        )

    def sends(h):
        return jnp.logical_and(j < times - 1, j >= h)

    def fwd_copy(i, d):
        return pltpu.make_async_remote_copy(
            src_ref=send1.at[i, d - 1],
            dst_ref=colp.at[i, :, pl.ds(pl.multiple_of(z * PIECE, PIECE), PIECE), :],
            send_sem=fwd_send.at[i, d - 1],
            recv_sem=fwd_recv.at[i, d - 1],
            device_id={"tile": partner(d)},
            device_id_type=MESH,
        )

    def fwd_arrival(i, d):
        return pltpu.make_async_remote_copy(
            src_ref=send1.at[i, d - 1],
            dst_ref=colp.at[i, :, pl.ds(pl.multiple_of(source(d) * PIECE, PIECE), PIECE), :],
            send_sem=fwd_send.at[i, d - 1],
            recv_sem=fwd_recv.at[i, d - 1],
            device_id={"tile": partner(d)},
            device_id_type=MESH,
        )

    @pl.when(sends(0))
    def _():
        hist_copy(0, 0).start()

    wide = (hops + 1) * span * GROUP
    out_pos = lax.broadcasted_iota(jnp.int32, (span * GROUP, wide), 0)
    in_pos = lax.broadcasted_iota(jnp.int32, (span * GROUP, wide), 1)
    lag = out_pos // GROUP + hops * span - in_pos // GROUP
    lag = jnp.where(out_pos % GROUP == in_pos % GROUP, lag, -1)
    tk[...] = lag.astype(jnp.float32)

    def tap_rows(n, _):
        here = pl.ds(pl.multiple_of(n * GROUP, GROUP), GROUP)
        lags = tk[here, :]
        values = jnp.zeros_like(lags)
        for k in range(tap_count):
            values = jnp.where(lags == float(k), taps[k], values)
        tk[here, :] = values
        return 0

    lax.fori_loop(0, span, tap_rows, 0)

    for h in range(hops):

        @pl.when(j <= h)
        def _(h=h):
            def clear(s, _):
                hist[h, s] = jnp.zeros((rows, side), hist.dtype)
                return 0

            lax.fori_loop(0, span, clear, 0)

    def clear_acc(s, _):
        acc[s] = jnp.zeros((side, cols), jnp.float32)
        return 0

    lax.fori_loop(0, span, clear_acc, 0)

    for load in loads:
        load.wait()

    def row_transform(i):
        for d in range(1, tiles):
            fwd_arrival(i, d).wait_recv()

        def frame(s, _):
            block = colp[i, s]
            for m in range(side // 256):
                here = slice(m * 256, (m + 1) * 256)
                basis = bp[here, pl.ds(pl.multiple_of(i * depth, depth), depth)]
                acc[s, here, :] += dot(basis, block)
            return 0

        lax.fori_loop(0, span, frame, 0)

    def forward(i, _):
        for h in range(hops):

            @pl.when(j > h)
            def _(h=h):
                hist_copy(h, i).wait_recv()

            if h + 1 < hops:

                @pl.when(sends(h + 1))
                def _(h=h):
                    hist_copy(h + 1, i).start()

        @pl.when(jnp.logical_and(sends(0), i < pieces - 1))
        def _():
            hist_copy(0, i + 1).start()

        matrix = tk[...].astype(jnp.bfloat16)

        def group(n, _):
            here = pl.ds(pl.multiple_of(i * PIECE + n * GROUP, GROUP), GROUP)
            blocks = [hist[h, :, here, :].reshape(span * GROUP, side) for h in reversed(range(hops))]
            blocks.append(x[:, here, :].reshape(span * GROUP, side))
            result = dot(matrix, jnp.concatenate(blocks, axis=0)).astype(jnp.bfloat16)
            flux[:, pl.ds(pl.multiple_of(n * GROUP, GROUP), GROUP), :] = result.reshape(span, GROUP, side)
            return 0

        lax.fori_loop(0, PIECE // GROUP, group, 0)

        for d in list(range(1, tiles)) + [0]:
            modes = pl.ds(pl.multiple_of(partner(d) * cols, cols), cols)
            result = dot(flux[...].reshape(span * PIECE, side), bt[:, modes]).astype(jnp.bfloat16)
            result = result.reshape(span, PIECE, cols)
            if d == 0:
                colp[i, :, pl.ds(pl.multiple_of(z * PIECE, PIECE), PIECE), :] = result
            else:
                send1[i, d - 1] = result
                fwd_copy(i, d).start()

        @pl.when(i > 0)
        def _():
            row_transform(i - 1)

        return 0

    def decay(n, _):
        here = pl.ds(pl.multiple_of(n * 64, 64), 64)
        retain[here, :] = jnp.exp(-retain[here, :])
        return 0

    lax.fori_loop(0, side // 64, decay, 0)
    lax.fori_loop(0, pieces, forward, 0)
    row_transform(pieces - 1)

    def close(n, _):
        here = pl.ds(pl.multiple_of(n * 64, 64), 64)
        rate = retain[here, :]
        last = acc[0, here, :]
        whole = rate * factor[0]
        for s in range(1, span):
            now = rate * factor[s]
            last = now * last + acc[s, here, :]
            whole = now * whole
        cout[here, :] = last
        dec[here, :] = whole
        return 0

    lax.fori_loop(0, side // 64, close, 0)

    share = side // CARRY_PIECES

    def carry_copy(q):
        here = pl.ds(q * share, share)
        return pltpu.make_async_remote_copy(
            src_ref=cout.at[here, :],
            dst_ref=carry.at[here, :],
            send_sem=carry_send.at[q],
            recv_sem=carry_recv.at[q],
            device_id={"tm": lax.rem(j + 1, times)},
            device_id_type=MESH,
        )

    @pl.when(j == 0)
    def _():
        carry[...] = jnp.zeros_like(carry)

    for q in range(CARRY_PIECES):

        @pl.when(j > 0)
        def _(q=q):
            carry_copy(q).wait_recv()
            here = pl.ds(q * share, share)
            cout[here, :] = dec[here, :] * carry[here, :] + cout[here, :]

        @pl.when(j < times - 1)
        def _(q=q):
            carry_copy(q).start()

    def inv_copy(s, d):
        return pltpu.make_async_remote_copy(
            src_ref=send2.at[s, d - 1],
            dst_ref=rowp.at[s, :, pl.ds(pl.multiple_of(z * cols, cols), cols)],
            send_sem=inv_send.at[s, d - 1],
            recv_sem=inv_recv.at[s, d - 1],
            device_id={"tile": partner(d)},
            device_id_type=MESH,
        )

    def inv_arrival(s, d):
        return pltpu.make_async_remote_copy(
            src_ref=send2.at[s, d - 1],
            dst_ref=rowp.at[s, :, pl.ds(pl.multiple_of(source(d) * cols, cols), cols)],
            send_sem=inv_send.at[s, d - 1],
            recv_sem=inv_recv.at[s, d - 1],
            device_id={"tile": partner(d)},
            device_id_type=MESH,
        )

    def inverse(s, _):
        fact = factor[s]

        def advance(n, _):
            here = pl.ds(pl.multiple_of(n * 128, 128), 128)
            now = (retain[here, :] * fact) * carry[here, :] + acc[s, here, :]
            carry[here, :] = now
            rb[here, :] = now.astype(jnp.bfloat16)
            return 0

        lax.fori_loop(0, side // 128, advance, 0)
        for d in list(range(1, tiles)) + [0]:
            mine = pl.ds(pl.multiple_of(partner(d) * rows, rows), rows)
            result = dot(bt[mine, :], rb[...]).astype(jnp.bfloat16)
            if d == 0:
                rowp[s, :, pl.ds(pl.multiple_of(z * cols, cols), cols)] = result
            else:
                send2[s, d - 1] = result
                inv_copy(s, d).start()
        return 0

    lax.fori_loop(0, span, inverse, 0)

    def finish(s, _):
        for d in range(1, tiles):
            inv_arrival(s, d).wait_recv()
        outv[s] = lax.dot_general(
            rowp[s], bt[...], (((1,), (1,)), ((), ())), preferred_element_type=jnp.float32
        ).astype(jnp.bfloat16)
        pltpu.make_async_copy(outv.at[s], out_hbm.at[s], out_sem.at[s]).start()
        return 0

    lax.fori_loop(0, span, finish, 0)

    def drain_frames(s, _):
        for d in range(1, tiles):
            inv_copy(s, d).wait_send()
        pltpu.make_async_copy(outv.at[s], out_hbm.at[s], out_sem.at[s]).wait()
        return 0

    lax.fori_loop(0, span, drain_frames, 0)

    def drain_pieces(i, _):
        for d in range(1, tiles):
            fwd_copy(i, d).wait_send()
        for h in range(hops):

            @pl.when(sends(h))
            def _(h=h):
                hist_copy(h, i).wait_send()

        return 0

    lax.fori_loop(0, pieces, drain_pieces, 0)

    @pl.when(j < times - 1)
    def _():
        for q in range(CARRY_PIECES):
            carry_copy(q).wait_send()


def on_device(frames, inverse_taps, mode_rate, frame_factor):
    span, rows, side = frames.shape
    tap_count = inverse_taps.shape[0]
    tiles = side // rows
    cols = side // tiles
    pieces = rows // PIECE
    depth = tiles * PIECE
    hops = min((tap_count - 1 + span - 1) // span, lax.axis_size("tm") - 1)
    index = jnp.arange(side, dtype=jnp.int32)
    place = index % depth
    cell = place // PIECE * rows + index // depth * PIECE + place % PIECE
    bt = cosine_values(index[None, :], index[:, None], side)
    bp = cosine_values(index[:, None], cell[None, :], side)
    any_space = pl.BlockSpec(memory_space=pl.ANY)
    smem = pl.BlockSpec(memory_space=pltpu.SMEM)
    b16, f32 = jnp.bfloat16, jnp.float32
    dma = pltpu.SemaphoreType.DMA
    return pl.pallas_call(
        kernel,
        out_shape=jax.ShapeDtypeStruct(frames.shape, b16),
        in_specs=[any_space, smem, any_space, smem, any_space, any_space],
        out_specs=any_space,
        scratch_shapes=[
            pltpu.VMEM((span, rows, side), b16),
            pltpu.VMEM((hops, span, rows, side), b16),
            pltpu.VMEM((side, side), b16),
            pltpu.VMEM((side, side), b16),
            pltpu.VMEM((side, cols), f32),
            pltpu.VMEM((span, PIECE, side), b16),
            pltpu.VMEM((pieces, tiles - 1, span, PIECE, cols), b16),
            pltpu.VMEM((pieces, span, depth, cols), b16),
            pltpu.VMEM((span, side, cols), f32),
            pltpu.VMEM((span * GROUP, (hops + 1) * span * GROUP), f32),
            pltpu.VMEM((side, cols), f32),
            pltpu.VMEM((side, cols), f32),
            pltpu.VMEM((side, cols), f32),
            pltpu.VMEM((side, cols), b16),
            pltpu.VMEM((span, tiles - 1, rows, cols), b16),
            pltpu.VMEM((span, rows, side), b16),
            pltpu.VMEM((span, rows, side), b16),
            dma((4,)),
            dma((hops, pieces)),
            dma((hops, pieces)),
            dma((pieces, tiles - 1)),
            dma((pieces, tiles - 1)),
            dma((CARRY_PIECES,)),
            dma((CARRY_PIECES,)),
            dma((span, tiles - 1)),
            dma((span, tiles - 1)),
            dma((span,)),
        ],
        compiler_params=pltpu.CompilerParams(
            collective_id=0, has_side_effects=True, vmem_limit_bytes=67043328
        ),
    )(frames, inverse_taps, mode_rate, frame_factor, bt, bp)


def solution(mesh):
    return jax.shard_map(
        on_device,
        mesh=mesh,
        in_specs=(P(("grp", "tm"), "tile", None), P(), P(None, "tile"), P(("grp", "tm"))),
        out_specs=P(("grp", "tm"), "tile", None),
        check_vma=False,
    )
```

```python
import jax
import jax.numpy as jnp
import numpy as np
from jax import lax
from jax.experimental import pallas as pl
from jax.experimental.pallas import tpu as pltpu
from jax.sharding import PartitionSpec as P

MESH = pl.DeviceIdType.MESH
GROUP = 16
PIECE = 32
RUN = 2
CARRY_PIECES = 4


def cosine_table(points):
    freq_idx = np.arange(points)[None, :]
    phase = (2 * np.arange(points)[:, None] + 1) * freq_idx % (4 * points)
    values = np.cos(np.pi * phase / (2.0 * points)) * np.sqrt(2.0 / points)
    values = np.where(freq_idx == 0, values / np.sqrt(2.0), values)
    return values.astype(np.float32).astype(jnp.bfloat16)


def dot(a, b):
    return jnp.dot(a, b, preferred_element_type=jnp.float32)


def kernel(
    x_hbm, taps, rate_hbm, factor, bt_hbm, out_hbm,
    x, hist, bt, bp, retain, flux, send1, colp, acc, tk, carry, cout, dec, rb, send2, rowp, outv,
    load_sem, hist_send, hist_recv, fwd_send, fwd_recv, carry_send, carry_recv,
    inv_send, inv_recv, out_sem,
):
    span, rows, side = x.shape
    hops = hist.shape[0]
    runs, _, depth, cols = colp.shape
    pieces = runs * RUN
    tap_count = taps.shape[0]
    tiles = side // rows
    times = lax.axis_size("tm")
    j = lax.axis_index("tm")
    z = lax.axis_index("tile")

    def partner(d):
        return lax.rem(z + d, tiles)

    def source(d):
        return lax.rem(z + tiles - d, tiles)

    loads = [
        pltpu.make_async_copy(src, dst, load_sem.at[n])
        for n, (src, dst) in enumerate(((x_hbm, x), (bt_hbm, bt), (rate_hbm, retain)))
    ]
    for load in loads:
        load.start()

    barrier = pltpu.get_barrier_semaphore()
    for d in range(1, tiles):
        pl.semaphore_signal(barrier, inc=1, device_id={"tile": partner(d)}, device_id_type=MESH)

    for other in (lax.rem(j + 1, times), lax.rem(j + times - 1, times)):
        pl.semaphore_signal(barrier, inc=1, device_id={"tm": other}, device_id_type=MESH)

    pl.semaphore_wait(barrier, tiles + 1)

    def piece_rows(i):
        return pl.ds(pl.multiple_of(i * PIECE, PIECE), PIECE)

    def landing(i, owner):
        offset = lax.rem(i, RUN) * (depth // RUN) + owner * PIECE
        return colp.at[i // RUN, :, pl.ds(pl.multiple_of(offset, PIECE), PIECE), :]

    def hist_copy(h, i):
        src = x_hbm if h == 0 else hist.at[h - 1]
        return pltpu.make_async_remote_copy(
            src_ref=src.at[:, piece_rows(i), :],
            dst_ref=hist.at[h, :, piece_rows(i), :],
            send_sem=hist_send.at[h, i],
            recv_sem=hist_recv.at[h, i],
            device_id={"tm": lax.rem(j + 1, times)},
            device_id_type=MESH,
        )

    def sends(h):
        return jnp.logical_and(j < times - 1, j >= h)

    def fwd_copy(i, d):
        return pltpu.make_async_remote_copy(
            src_ref=send1.at[i, d - 1],
            dst_ref=landing(i, z),
            send_sem=fwd_send.at[i, d - 1],
            recv_sem=fwd_recv.at[i, d - 1],
            device_id={"tile": partner(d)},
            device_id_type=MESH,
        )

    def fwd_arrival(i, d):
        return pltpu.make_async_remote_copy(
            src_ref=send1.at[i, d - 1],
            dst_ref=landing(i, source(d)),
            send_sem=fwd_send.at[i, d - 1],
            recv_sem=fwd_recv.at[i, d - 1],
            device_id={"tile": partner(d)},
            device_id_type=MESH,
        )

    @pl.when(sends(0))
    def _():
        hist_copy(0, 0).start()

    wide = (hops + 1) * span * GROUP
    out_pos = lax.broadcasted_iota(jnp.int32, (span * GROUP, wide), 0)
    in_pos = lax.broadcasted_iota(jnp.int32, (span * GROUP, wide), 1)
    lag = out_pos // GROUP + hops * span - in_pos // GROUP
    lag = jnp.where(out_pos % GROUP == in_pos % GROUP, lag, -1)
    tk[...] = lag.astype(jnp.float32)

    def tap_rows(n, _):
        here = pl.ds(pl.multiple_of(n * GROUP, GROUP), GROUP)
        lags = tk[here, :]
        values = jnp.zeros_like(lags)
        for k in range(tap_count):
            values = jnp.where(lags == float(k), taps[k], values)
        tk[here, :] = values
        return 0

    lax.fori_loop(0, span, tap_rows, 0)

    for h in range(hops):

        @pl.when(j <= h)
        def _(h=h):
            def clear(s, _):
                hist[h, s] = jnp.zeros((rows, side), hist.dtype)
                return 0

            lax.fori_loop(0, span, clear, 0)

    def clear_acc(s, _):
        acc[s] = jnp.zeros((side, cols), jnp.float32)
        return 0

    lax.fori_loop(0, span, clear_acc, 0)

    for load in loads:
        load.wait()

    def row_transform(n):
        pixels = [
            bt[pl.ds(pl.multiple_of(owner * rows + (n * RUN + part) * PIECE, PIECE), PIECE), :]
            for part in range(RUN)
            for owner in range(tiles)
        ]
        bp[...] = jnp.concatenate(pixels, axis=0).T
        for part in range(RUN):
            for d in range(1, tiles):
                fwd_arrival(n * RUN + part, d).wait_recv()

        def frame(s, _):
            block = colp[n, s]
            for m in range(side // 256):
                here = slice(m * 256, (m + 1) * 256)
                acc[s, here, :] += dot(bp[here, :], block)
            return 0

        lax.fori_loop(0, span, frame, 0)

    def forward(i, _):
        for h in range(hops):

            @pl.when(j > h)
            def _(h=h):
                hist_copy(h, i).wait_recv()

            if h + 1 < hops:

                @pl.when(sends(h + 1))
                def _(h=h):
                    hist_copy(h + 1, i).start()

        @pl.when(jnp.logical_and(sends(0), i < pieces - 1))
        def _():
            hist_copy(0, i + 1).start()

        matrix = tk[...].astype(jnp.bfloat16)

        def group(n, _):
            here = pl.ds(pl.multiple_of(i * PIECE + n * GROUP, GROUP), GROUP)
            blocks = [hist[h, :, here, :].reshape(span * GROUP, side) for h in reversed(range(hops))]
            blocks.append(x[:, here, :].reshape(span * GROUP, side))
            result = dot(matrix, jnp.concatenate(blocks, axis=0)).astype(jnp.bfloat16)
            flux[:, pl.ds(pl.multiple_of(n * GROUP, GROUP), GROUP), :] = result.reshape(span, GROUP, side)
            return 0

        lax.fori_loop(0, PIECE // GROUP, group, 0)

        for d in list(range(1, tiles)) + [0]:
            modes = pl.ds(pl.multiple_of(partner(d) * cols, cols), cols)
            result = dot(flux[...].reshape(span * PIECE, side), bt[:, modes]).astype(jnp.bfloat16)
            result = result.reshape(span, PIECE, cols)
            if d == 0:
                landing(i, z)[...] = result
            else:
                send1[i, d - 1] = result
                fwd_copy(i, d).start()

        @pl.when(jnp.logical_and(lax.rem(i, RUN) == RUN - 1, i >= RUN))
        def _():
            row_transform(i // RUN - 1)

        return 0

    def decay(n, _):
        here = pl.ds(pl.multiple_of(n * 64, 64), 64)
        retain[here, :] = jnp.exp(-retain[here, :])
        return 0

    lax.fori_loop(0, side // 64, decay, 0)
    lax.fori_loop(0, pieces, forward, 0)
    row_transform(runs - 1)

    def close(n, _):
        here = pl.ds(pl.multiple_of(n * 64, 64), 64)
        rate = retain[here, :]
        last = acc[0, here, :]
        whole = rate * factor[0]
        for s in range(1, span):
            now = rate * factor[s]
            last = now * last + acc[s, here, :]
            whole = now * whole
        cout[here, :] = last
        dec[here, :] = whole
        return 0

    lax.fori_loop(0, side // 64, close, 0)

    share = side // CARRY_PIECES

    def carry_copy(q):
        here = pl.ds(q * share, share)
        return pltpu.make_async_remote_copy(
            src_ref=cout.at[here, :],
            dst_ref=carry.at[here, :],
            send_sem=carry_send.at[q],
            recv_sem=carry_recv.at[q],
            device_id={"tm": lax.rem(j + 1, times)},
            device_id_type=MESH,
        )

    @pl.when(j == 0)
    def _():
        carry[...] = jnp.zeros_like(carry)

    for q in range(CARRY_PIECES):

        @pl.when(j > 0)
        def _(q=q):
            carry_copy(q).wait_recv()
            here = pl.ds(q * share, share)
            cout[here, :] = dec[here, :] * carry[here, :] + cout[here, :]

        @pl.when(j < times - 1)
        def _(q=q):
            carry_copy(q).start()

    def inv_copy(s, d):
        return pltpu.make_async_remote_copy(
            src_ref=send2.at[s, d - 1],
            dst_ref=rowp.at[s, :, pl.ds(pl.multiple_of(z * cols, cols), cols)],
            send_sem=inv_send.at[s, d - 1],
            recv_sem=inv_recv.at[s, d - 1],
            device_id={"tile": partner(d)},
            device_id_type=MESH,
        )

    def inv_arrival(s, d):
        return pltpu.make_async_remote_copy(
            src_ref=send2.at[s, d - 1],
            dst_ref=rowp.at[s, :, pl.ds(pl.multiple_of(source(d) * cols, cols), cols)],
            send_sem=inv_send.at[s, d - 1],
            recv_sem=inv_recv.at[s, d - 1],
            device_id={"tile": partner(d)},
            device_id_type=MESH,
        )

    def inverse(s, _):
        fact = factor[s]

        def advance(n, _):
            here = pl.ds(pl.multiple_of(n * 128, 128), 128)
            now = (retain[here, :] * fact) * carry[here, :] + acc[s, here, :]
            carry[here, :] = now
            rb[here, :] = now.astype(jnp.bfloat16)
            return 0

        lax.fori_loop(0, side // 128, advance, 0)
        for d in list(range(1, tiles)) + [0]:
            mine = pl.ds(pl.multiple_of(partner(d) * rows, rows), rows)
            result = dot(bt[mine, :], rb[...]).astype(jnp.bfloat16)
            if d == 0:
                rowp[s, :, pl.ds(pl.multiple_of(z * cols, cols), cols)] = result
            else:
                send2[s, d - 1] = result
                inv_copy(s, d).start()
        return 0

    lax.fori_loop(0, span, inverse, 0)

    def finish(s, _):
        for d in range(1, tiles):
            inv_arrival(s, d).wait_recv()
        outv[s] = lax.dot_general(
            rowp[s], bt[...], (((1,), (1,)), ((), ())), preferred_element_type=jnp.float32
        ).astype(jnp.bfloat16)
        pltpu.make_async_copy(outv.at[s], out_hbm.at[s], out_sem.at[s]).start()
        return 0

    lax.fori_loop(0, span, finish, 0)

    def drain_frames(s, _):
        for d in range(1, tiles):
            inv_copy(s, d).wait_send()
        pltpu.make_async_copy(outv.at[s], out_hbm.at[s], out_sem.at[s]).wait()
        return 0

    lax.fori_loop(0, span, drain_frames, 0)

    def drain_pieces(i, _):
        for d in range(1, tiles):
            fwd_copy(i, d).wait_send()
        for h in range(hops):

            @pl.when(sends(h))
            def _(h=h):
                hist_copy(h, i).wait_send()

        return 0

    lax.fori_loop(0, pieces, drain_pieces, 0)

    @pl.when(j < times - 1)
    def _():
        for q in range(CARRY_PIECES):
            carry_copy(q).wait_send()


def on_device(frames, inverse_taps, mode_rate, frame_factor):
    span, rows, side = frames.shape
    tap_count = inverse_taps.shape[0]
    tiles = side // rows
    cols = side // tiles
    pieces = rows // PIECE
    depth = tiles * PIECE * RUN
    hops = min((tap_count - 1 + span - 1) // span, lax.axis_size("tm") - 1)
    bt = jnp.asarray(cosine_table(side))
    any_space = pl.BlockSpec(memory_space=pl.ANY)
    smem = pl.BlockSpec(memory_space=pltpu.SMEM)
    b16, f32 = jnp.bfloat16, jnp.float32
    dma = pltpu.SemaphoreType.DMA
    return pl.pallas_call(
        kernel,
        out_shape=jax.ShapeDtypeStruct(frames.shape, b16),
        in_specs=[any_space, smem, any_space, smem, any_space],
        out_specs=any_space,
        scratch_shapes=[
            pltpu.VMEM((span, rows, side), b16),
            pltpu.VMEM((hops, span, rows, side), b16),
            pltpu.VMEM((side, side), b16),
            pltpu.VMEM((side, depth), b16),
            pltpu.VMEM((side, cols), f32),
            pltpu.VMEM((span, PIECE, side), b16),
            pltpu.VMEM((pieces, tiles - 1, span, PIECE, cols), b16),
            pltpu.VMEM((pieces // RUN, span, depth, cols), b16),
            pltpu.VMEM((span, side, cols), f32),
            pltpu.VMEM((span * GROUP, (hops + 1) * span * GROUP), f32),
            pltpu.VMEM((side, cols), f32),
            pltpu.VMEM((side, cols), f32),
            pltpu.VMEM((side, cols), f32),
            pltpu.VMEM((side, cols), b16),
            pltpu.VMEM((span, tiles - 1, rows, cols), b16),
            pltpu.VMEM((span, rows, side), b16),
            pltpu.VMEM((span, rows, side), b16),
            dma((3,)),
            dma((hops, pieces)),
            dma((hops, pieces)),
            dma((pieces, tiles - 1)),
            dma((pieces, tiles - 1)),
            dma((CARRY_PIECES,)),
            dma((CARRY_PIECES,)),
            dma((span, tiles - 1)),
            dma((span, tiles - 1)),
            dma((span,)),
        ],
        compiler_params=pltpu.CompilerParams(
            collective_id=0, has_side_effects=True, vmem_limit_bytes=67043328
        ),
    )(frames, inverse_taps, mode_rate, frame_factor, bt)


def solution(mesh):
    return jax.shard_map(
        on_device,
        mesh=mesh,
        in_specs=(P(("grp", "tm"), "tile", None), P(), P(None, "tile"), P(("grp", "tm"))),
        out_specs=P(("grp", "tm"), "tile", None),
        check_vma=False,
    )
```

```python
import jax
import jax.numpy as jnp
import numpy as np
from jax import lax
from jax.experimental import pallas as pl
from jax.experimental.pallas import tpu as pltpu
from jax.sharding import PartitionSpec as P

MESH = pl.DeviceIdType.MESH
GROUP = 16
PIECE = 32
RUN = 2
CARRY_PIECES = 4


def cosine_table(points):
    freq_idx = np.arange(points)[None, :]
    phase = (2 * np.arange(points)[:, None] + 1) * freq_idx % (4 * points)
    values = np.cos(np.pi * phase / (2.0 * points)) * np.sqrt(2.0 / points)
    values = np.where(freq_idx == 0, values / np.sqrt(2.0), values)
    return values.astype(np.float32).astype(jnp.bfloat16)


def dot(a, b):
    return jnp.dot(a, b, preferred_element_type=jnp.float32)


def kernel(
    x_hbm, taps, rate_hbm, factor, bt_hbm, out_hbm,
    x, hist, bt, bp, retain, flux, send1, colp, acc, tk, carry, cout, dec, rb, send2, rowp,
    load_sem, hist_send, hist_recv, fwd_send, fwd_recv, carry_send, carry_recv,
    inv_send, inv_recv, out_sem,
):
    span, rows, side = x.shape
    hops = hist.shape[0]
    runs, _, depth, cols = colp.shape
    pieces = runs * RUN
    tap_count = taps.shape[0]
    tiles = side // rows
    times = lax.axis_size("tm")
    j = lax.axis_index("tm")
    z = lax.axis_index("tile")

    def partner(d):
        return lax.rem(z + d, tiles)

    def source(d):
        return lax.rem(z + tiles - d, tiles)

    loads = [
        pltpu.make_async_copy(src, dst, load_sem.at[n])
        for n, (src, dst) in enumerate(((x_hbm, x), (bt_hbm, bt), (rate_hbm, retain)))
    ]
    for load in loads:
        load.start()

    barrier = pltpu.get_barrier_semaphore()
    for d in range(1, tiles):
        pl.semaphore_signal(barrier, inc=1, device_id={"tile": partner(d)}, device_id_type=MESH)

    for other in (lax.rem(j + 1, times), lax.rem(j + times - 1, times)):
        pl.semaphore_signal(barrier, inc=1, device_id={"tm": other}, device_id_type=MESH)

    pl.semaphore_wait(barrier, tiles + 1)

    def piece_rows(i):
        return pl.ds(pl.multiple_of(i * PIECE, PIECE), PIECE)

    def landing(i, owner):
        offset = lax.rem(i, RUN) * (depth // RUN) + owner * PIECE
        return colp.at[i // RUN, :, pl.ds(pl.multiple_of(offset, PIECE), PIECE), :]

    def hist_copy(h, i):
        src = x_hbm if h == 0 else hist.at[h - 1]
        return pltpu.make_async_remote_copy(
            src_ref=src.at[:, piece_rows(i), :],
            dst_ref=hist.at[h, :, piece_rows(i), :],
            send_sem=hist_send.at[h, i],
            recv_sem=hist_recv.at[h, i],
            device_id={"tm": lax.rem(j + 1, times)},
            device_id_type=MESH,
        )

    def sends(h):
        return jnp.logical_and(j < times - 1, j >= h)

    def fwd_copy(i, d):
        return pltpu.make_async_remote_copy(
            src_ref=send1.at[i, d - 1],
            dst_ref=landing(i, z),
            send_sem=fwd_send.at[i, d - 1],
            recv_sem=fwd_recv.at[i, d - 1],
            device_id={"tile": partner(d)},
            device_id_type=MESH,
        )

    def fwd_arrival(i, d):
        return pltpu.make_async_remote_copy(
            src_ref=send1.at[i, d - 1],
            dst_ref=landing(i, source(d)),
            send_sem=fwd_send.at[i, d - 1],
            recv_sem=fwd_recv.at[i, d - 1],
            device_id={"tile": partner(d)},
            device_id_type=MESH,
        )

    @pl.when(sends(0))
    def _():
        hist_copy(0, 0).start()

    wide = (hops + 1) * span * GROUP
    out_pos = lax.broadcasted_iota(jnp.int32, (span * GROUP, wide), 0)
    in_pos = lax.broadcasted_iota(jnp.int32, (span * GROUP, wide), 1)
    lag = out_pos // GROUP + hops * span - in_pos // GROUP
    lag = jnp.where(out_pos % GROUP == in_pos % GROUP, lag, -1)
    tk[...] = lag.astype(jnp.float32)

    def tap_rows(n, _):
        here = pl.ds(pl.multiple_of(n * GROUP, GROUP), GROUP)
        lags = tk[here, :]
        values = jnp.zeros_like(lags)
        for k in range(tap_count):
            values = jnp.where(lags == float(k), taps[k], values)
        tk[here, :] = values
        return 0

    lax.fori_loop(0, span, tap_rows, 0)

    loads[0].wait()
    loads[1].wait()

    def row_setup(n):
        pixels = [
            bt[pl.ds(pl.multiple_of(owner * rows + (n * RUN + part) * PIECE, PIECE), PIECE), :]
            for part in range(RUN)
            for owner in range(tiles)
        ]
        bp[...] = jnp.concatenate(pixels, axis=0).T
        for part in range(RUN):
            for d in range(1, tiles):
                fwd_arrival(n * RUN + part, d).wait_recv()

    def row_frames(n, first, start):
        def frame(s, _):
            block = colp[n, s]
            for m in range(side // 256):
                here = slice(m * 256, (m + 1) * 256)
                share = dot(bp[here, :], block)
                acc[s, here, :] = share if first else acc[s, here, :] + share
            return 0

        lax.fori_loop(start, span, frame, 0)

    def decay(n, _):
        here = pl.ds(pl.multiple_of(n * 64, 64), 64)
        retain[here, :] = jnp.exp(-retain[here, :])
        return 0

    def forward(i, _):
        for h in range(hops):

            @pl.when(j > h)
            def _(h=h):
                hist_copy(h, i).wait_recv()

            @pl.when(j <= h)
            def _(h=h):
                hist[h, :, piece_rows(i), :] = jnp.zeros((span, PIECE, side), hist.dtype)

            if h + 1 < hops:

                @pl.when(sends(h + 1))
                def _(h=h):
                    hist_copy(h + 1, i).start()

        @pl.when(jnp.logical_and(sends(0), i < pieces - 1))
        def _():
            hist_copy(0, i + 1).start()

        matrix = tk[...].astype(jnp.bfloat16)

        def group(n, _):
            here = pl.ds(pl.multiple_of(i * PIECE + n * GROUP, GROUP), GROUP)
            blocks = [hist[h, :, here, :].reshape(span * GROUP, side) for h in reversed(range(hops))]
            blocks.append(x[:, here, :].reshape(span * GROUP, side))
            result = dot(matrix, jnp.concatenate(blocks, axis=0)).astype(jnp.bfloat16)
            flux[:, pl.ds(pl.multiple_of(n * GROUP, GROUP), GROUP), :] = result.reshape(span, GROUP, side)
            return 0

        lax.fori_loop(0, PIECE // GROUP, group, 0)

        for d in list(range(1, tiles)) + [0]:
            modes = pl.ds(pl.multiple_of(partner(d) * cols, cols), cols)
            result = dot(flux[...].reshape(span * PIECE, side), bt[:, modes]).astype(jnp.bfloat16)
            result = result.reshape(span, PIECE, cols)
            if d == 0:
                landing(i, z)[...] = result
            else:
                send1[i, d - 1] = result
                fwd_copy(i, d).start()

        @pl.when(jnp.logical_and(lax.rem(i, RUN) == RUN - 1, i >= RUN))
        def _():
            n = i // RUN - 1
            row_setup(n)

            @pl.when(n == 0)
            def _():
                row_frames(n, True, 0)

            @pl.when(n > 0)
            def _():
                row_frames(n, False, 0)

        @pl.when(i == pieces - 1)
        def _():
            loads[2].wait()
            lax.fori_loop(0, side // 64, decay, 0)

        return 0

    lax.fori_loop(0, pieces, forward, 0)
    row_setup(runs - 1)

    def close(n, _):
        here = pl.ds(pl.multiple_of(n * 64, 64), 64)
        rate = retain[here, :]
        last = acc[0, here, :]
        whole = rate * factor[0]
        for s in range(1, span):
            now = rate * factor[s]
            last = now * last + acc[s, here, :]
            whole = now * whole
        cout[here, :] = last
        dec[here, :] = whole
        return 0

    def close_exact(n, _):
        here = pl.ds(pl.multiple_of(n * 64, 64), 64)
        rate = retain[here, :]
        last = carry[here, :]
        for s in range(1, span):
            last = (rate * factor[s]) * last + acc[s, here, :]
        cout[here, :] = last
        return 0

    share = side // CARRY_PIECES

    def carry_copy(q):
        here = pl.ds(q * share, share)
        return pltpu.make_async_remote_copy(
            src_ref=cout.at[here, :],
            dst_ref=carry.at[here, :],
            send_sem=carry_send.at[q],
            recv_sem=carry_recv.at[q],
            device_id={"tm": lax.rem(j + 1, times)},
            device_id_type=MESH,
        )

    def inv_copy(s, d):
        return pltpu.make_async_remote_copy(
            src_ref=send2.at[s, d - 1],
            dst_ref=rowp.at[s, :, pl.ds(pl.multiple_of(z * cols, cols), cols)],
            send_sem=inv_send.at[s, d - 1],
            recv_sem=inv_recv.at[s, d - 1],
            device_id={"tile": partner(d)},
            device_id_type=MESH,
        )

    def inv_arrival(s, d):
        return pltpu.make_async_remote_copy(
            src_ref=send2.at[s, d - 1],
            dst_ref=rowp.at[s, :, pl.ds(pl.multiple_of(source(d) * cols, cols), cols)],
            send_sem=inv_send.at[s, d - 1],
            recv_sem=inv_recv.at[s, d - 1],
            device_id={"tile": partner(d)},
            device_id_type=MESH,
        )

    def inverse(s, _):
        fact = factor[s]

        def advance(n, _):
            here = pl.ds(pl.multiple_of(n * 128, 128), 128)
            now = (retain[here, :] * fact) * carry[here, :] + acc[s, here, :]
            carry[here, :] = now
            rb[here, :] = now.astype(jnp.bfloat16)
            return 0

        lax.fori_loop(0, side // 128, advance, 0)
        for d in list(range(1, tiles)) + [0]:
            mine = pl.ds(pl.multiple_of(partner(d) * rows, rows), rows)
            result = dot(bt[mine, :], rb[...]).astype(jnp.bfloat16)
            if d == 0:
                rowp[s, :, pl.ds(pl.multiple_of(z * cols, cols), cols)] = result
            else:
                send2[s, d - 1] = result
                inv_copy(s, d).start()
        return 0

    early = lax.rem(j, 2) == 0
    last_first = runs == 1

    @pl.when(early)
    def _():
        @pl.when(j == 0)
        def _():
            carry[...] = jnp.zeros_like(carry)

        row_frame_0 = colp[runs - 1, 0]
        for m in range(side // 256):
            here = slice(m * 256, (m + 1) * 256)
            part = dot(bp[here, :], row_frame_0)
            acc[0, here, :] = part if last_first else acc[0, here, :] + part

        @pl.when(j > 0)
        def _():
            for q in range(CARRY_PIECES):
                carry_copy(q).wait_recv()

        inverse(0, 0)
        row_frames(runs - 1, last_first, 1)
        for q in range(CARRY_PIECES):
            lax.fori_loop(q * share // 64, (q + 1) * share // 64, close_exact, 0)

            @pl.when(j < times - 1)
            def _(q=q):
                carry_copy(q).start()

        lax.fori_loop(1, span, inverse, 0)

    @pl.when(jnp.logical_not(early))
    def _():
        row_frames(runs - 1, last_first, 0)
        lax.fori_loop(0, side // 64, close, 0)
        for q in range(CARRY_PIECES):
            carry_copy(q).wait_recv()
            here = pl.ds(q * share, share)
            cout[here, :] = dec[here, :] * carry[here, :] + cout[here, :]

            @pl.when(j < times - 1)
            def _(q=q):
                carry_copy(q).start()

        lax.fori_loop(0, span, inverse, 0)

    def finish(s, _):
        for d in range(1, tiles):
            inv_arrival(s, d).wait_recv()
        x[s] = lax.dot_general(
            rowp[s], bt[...], (((1,), (1,)), ((), ())), preferred_element_type=jnp.float32
        ).astype(jnp.bfloat16)
        pltpu.make_async_copy(x.at[s], out_hbm.at[s], out_sem.at[s]).start()
        return 0

    lax.fori_loop(0, span, finish, 0)

    def drain_frames(s, _):
        for d in range(1, tiles):
            inv_copy(s, d).wait_send()
        pltpu.make_async_copy(x.at[s], out_hbm.at[s], out_sem.at[s]).wait()
        return 0

    lax.fori_loop(0, span, drain_frames, 0)

    def drain_pieces(i, _):
        for d in range(1, tiles):
            fwd_copy(i, d).wait_send()
        for h in range(hops):

            @pl.when(sends(h))
            def _(h=h):
                hist_copy(h, i).wait_send()

        return 0

    lax.fori_loop(0, pieces, drain_pieces, 0)

    @pl.when(j < times - 1)
    def _():
        for q in range(CARRY_PIECES):
            carry_copy(q).wait_send()


def on_device(frames, inverse_taps, mode_rate, frame_factor):
    span, rows, side = frames.shape
    tap_count = inverse_taps.shape[0]
    tiles = side // rows
    cols = side // tiles
    pieces = rows // PIECE
    depth = tiles * PIECE * RUN
    hops = min((tap_count - 1 + span - 1) // span, lax.axis_size("tm") - 1)
    bt = jnp.asarray(cosine_table(side))
    any_space = pl.BlockSpec(memory_space=pl.ANY)
    smem = pl.BlockSpec(memory_space=pltpu.SMEM)
    b16, f32 = jnp.bfloat16, jnp.float32
    dma = pltpu.SemaphoreType.DMA
    return pl.pallas_call(
        kernel,
        out_shape=jax.ShapeDtypeStruct(frames.shape, b16),
        in_specs=[any_space, smem, any_space, smem, any_space],
        out_specs=any_space,
        scratch_shapes=[
            pltpu.VMEM((span, rows, side), b16),
            pltpu.VMEM((hops, span, rows, side), b16),
            pltpu.VMEM((side, side), b16),
            pltpu.VMEM((side, depth), b16),
            pltpu.VMEM((side, cols), f32),
            pltpu.VMEM((span, PIECE, side), b16),
            pltpu.VMEM((pieces, tiles - 1, span, PIECE, cols), b16),
            pltpu.VMEM((pieces // RUN, span, depth, cols), b16),
            pltpu.VMEM((span, side, cols), f32),
            pltpu.VMEM((span * GROUP, (hops + 1) * span * GROUP), f32),
            pltpu.VMEM((side, cols), f32),
            pltpu.VMEM((side, cols), f32),
            pltpu.VMEM((side, cols), f32),
            pltpu.VMEM((side, cols), b16),
            pltpu.VMEM((span, tiles - 1, rows, cols), b16),
            pltpu.VMEM((span, rows, side), b16),
            dma((3,)),
            dma((hops, pieces)),
            dma((hops, pieces)),
            dma((pieces, tiles - 1)),
            dma((pieces, tiles - 1)),
            dma((CARRY_PIECES,)),
            dma((CARRY_PIECES,)),
            dma((span, tiles - 1)),
            dma((span, tiles - 1)),
            dma((span,)),
        ],
        compiler_params=pltpu.CompilerParams(
            collective_id=0, has_side_effects=True, vmem_limit_bytes=67043328
        ),
    )(frames, inverse_taps, mode_rate, frame_factor, bt)


def solution(mesh):
    return jax.shard_map(
        on_device,
        mesh=mesh,
        in_specs=(P(("grp", "tm"), "tile", None), P(), P(None, "tile"), P(("grp", "tm"))),
        out_specs=P(("grp", "tm"), "tile", None),
        check_vma=False,
    )
```

```python
import jax
import jax.numpy as jnp
import numpy as np
from jax import lax
from jax.experimental import pallas as pl
from jax.experimental.pallas import tpu as pltpu
from jax.sharding import PartitionSpec as P

MESH = pl.DeviceIdType.MESH
GROUP = 16
PIECE = 32
RUN = 2
CARRY_PIECES = 4


def cosine_table(points):
    freq_idx = np.arange(points)[None, :]
    phase = (2 * np.arange(points)[:, None] + 1) * freq_idx % (4 * points)
    values = np.cos(np.pi * phase / (2.0 * points)) * np.sqrt(2.0 / points)
    values = np.where(freq_idx == 0, values / np.sqrt(2.0), values)
    return values.astype(np.float32).astype(jnp.bfloat16)


def dot(a, b):
    return jnp.dot(a, b, preferred_element_type=jnp.float32)


def kernel(
    x_hbm, taps, rate_hbm, factor, bt_hbm, out_hbm,
    x, hist, bt, bp, retain, flux, send1, colp, acc, tk, carry, came, cout, dec, rb, send2, rowp,
    load_sem, hist_send, hist_recv, fwd_send, fwd_recv, carry_send, carry_recv,
    inv_send, inv_recv, out_sem,
):
    span, rows, side = x.shape
    hops = hist.shape[0]
    runs, _, depth, cols = colp.shape
    pieces = runs * RUN
    tap_count = taps.shape[0]
    tiles = side // rows
    times = lax.axis_size("tm")
    j = lax.axis_index("tm")
    z = lax.axis_index("tile")

    def partner(d):
        return lax.rem(z + d, tiles)

    def source(d):
        return lax.rem(z + tiles - d, tiles)

    loads = [
        pltpu.make_async_copy(src, dst, load_sem.at[n])
        for n, (src, dst) in enumerate(((x_hbm, x), (bt_hbm, bt), (rate_hbm, retain)))
    ]
    for load in loads:
        load.start()

    barrier = pltpu.get_barrier_semaphore()
    for d in range(1, tiles):
        pl.semaphore_signal(barrier, inc=1, device_id={"tile": partner(d)}, device_id_type=MESH)

    for other in (lax.rem(j + 1, times), lax.rem(j + times - 1, times)):
        pl.semaphore_signal(barrier, inc=1, device_id={"tm": other}, device_id_type=MESH)

    pl.semaphore_wait(barrier, tiles + 1)

    def piece_rows(i):
        return pl.ds(pl.multiple_of(i * PIECE, PIECE), PIECE)

    def landing(i, owner):
        offset = lax.rem(i, RUN) * (depth // RUN) + owner * PIECE
        return colp.at[i // RUN, :, pl.ds(pl.multiple_of(offset, PIECE), PIECE), :]

    def hist_copy(h, i):
        src = x_hbm if h == 0 else hist.at[h - 1]
        return pltpu.make_async_remote_copy(
            src_ref=src.at[:, piece_rows(i), :],
            dst_ref=hist.at[h, :, piece_rows(i), :],
            send_sem=hist_send.at[h, i],
            recv_sem=hist_recv.at[h, i],
            device_id={"tm": lax.rem(j + 1, times)},
            device_id_type=MESH,
        )

    def sends(h):
        return jnp.logical_and(j < times - 1, j >= h)

    def fwd_copy(i, d):
        return pltpu.make_async_remote_copy(
            src_ref=send1.at[i, d - 1],
            dst_ref=landing(i, z),
            send_sem=fwd_send.at[i, d - 1],
            recv_sem=fwd_recv.at[i, d - 1],
            device_id={"tile": partner(d)},
            device_id_type=MESH,
        )

    def fwd_arrival(i, d):
        return pltpu.make_async_remote_copy(
            src_ref=send1.at[i, d - 1],
            dst_ref=landing(i, source(d)),
            send_sem=fwd_send.at[i, d - 1],
            recv_sem=fwd_recv.at[i, d - 1],
            device_id={"tile": partner(d)},
            device_id_type=MESH,
        )

    @pl.when(sends(0))
    def _():
        hist_copy(0, 0).start()

    wide = (hops + 1) * span * GROUP
    out_pos = lax.broadcasted_iota(jnp.int32, (span * GROUP, wide), 0)
    in_pos = lax.broadcasted_iota(jnp.int32, (span * GROUP, wide), 1)
    lag = out_pos // GROUP + hops * span - in_pos // GROUP
    lag = jnp.where(out_pos % GROUP == in_pos % GROUP, lag, -1)
    tk[...] = lag.astype(jnp.float32)

    def tap_rows(n, _):
        here = pl.ds(pl.multiple_of(n * GROUP, GROUP), GROUP)
        lags = tk[here, :]
        values = jnp.zeros_like(lags)
        for k in range(tap_count):
            values = jnp.where(lags == float(k), taps[k], values)
        tk[here, :] = values
        return 0

    lax.fori_loop(0, span, tap_rows, 0)

    loads[0].wait()
    loads[1].wait()

    def row_setup(n):
        pixels = [
            bt[pl.ds(pl.multiple_of(owner * rows + (n * RUN + part) * PIECE, PIECE), PIECE), :]
            for part in range(RUN)
            for owner in range(tiles)
        ]
        bp[...] = jnp.concatenate(pixels, axis=0).T
        for part in range(RUN):
            for d in range(1, tiles):
                fwd_arrival(n * RUN + part, d).wait_recv()

    def row_frames(n, first, start):
        def frame(s, _):
            block = colp[n, s]
            for m in range(side // 256):
                here = slice(m * 256, (m + 1) * 256)
                share = dot(bp[here, :], block)
                acc[s, here, :] = share if first else acc[s, here, :] + share
            return 0

        lax.fori_loop(start, span, frame, 0)

    def decay(n, _):
        here = pl.ds(pl.multiple_of(n * 64, 64), 64)
        retain[here, :] = jnp.exp(-retain[here, :])
        return 0

    def forward(i, _):
        for h in range(hops):

            @pl.when(j > h)
            def _(h=h):
                hist_copy(h, i).wait_recv()

            @pl.when(j <= h)
            def _(h=h):
                hist[h, :, piece_rows(i), :] = jnp.zeros((span, PIECE, side), hist.dtype)

            if h + 1 < hops:

                @pl.when(sends(h + 1))
                def _(h=h):
                    hist_copy(h + 1, i).start()

        @pl.when(jnp.logical_and(sends(0), i < pieces - 1))
        def _():
            hist_copy(0, i + 1).start()

        matrix = tk[...].astype(jnp.bfloat16)

        def group(n, _):
            here = pl.ds(pl.multiple_of(i * PIECE + n * GROUP, GROUP), GROUP)
            blocks = [hist[h, :, here, :].reshape(span * GROUP, side) for h in reversed(range(hops))]
            blocks.append(x[:, here, :].reshape(span * GROUP, side))
            result = dot(matrix, jnp.concatenate(blocks, axis=0)).astype(jnp.bfloat16)
            flux[:, pl.ds(pl.multiple_of(n * GROUP, GROUP), GROUP), :] = result.reshape(span, GROUP, side)
            return 0

        lax.fori_loop(0, PIECE // GROUP, group, 0)

        for d in list(range(1, tiles)) + [0]:
            modes = pl.ds(pl.multiple_of(partner(d) * cols, cols), cols)
            result = dot(flux[...].reshape(span * PIECE, side), bt[:, modes]).astype(jnp.bfloat16)
            result = result.reshape(span, PIECE, cols)
            if d == 0:
                landing(i, z)[...] = result
            else:
                send1[i, d - 1] = result
                fwd_copy(i, d).start()

        @pl.when(jnp.logical_and(lax.rem(i, RUN) == RUN - 1, i >= RUN))
        def _():
            n = i // RUN - 1
            row_setup(n)

            @pl.when(n == 0)
            def _():
                row_frames(n, True, 0)

            @pl.when(n > 0)
            def _():
                row_frames(n, False, 0)

        @pl.when(i == pieces - 1)
        def _():
            loads[2].wait()
            lax.fori_loop(0, side // 64, decay, 0)

        return 0

    lax.fori_loop(0, pieces, forward, 0)
    row_setup(runs - 1)

    def close(n, _):
        here = pl.ds(pl.multiple_of(n * 64, 64), 64)
        rate = retain[here, :]
        last = acc[0, here, :]
        whole = rate * factor[0]
        for s in range(1, span):
            now = rate * factor[s]
            last = now * last + acc[s, here, :]
            whole = now * whole
        carry[here, :] = last
        dec[here, :] = whole
        return 0

    def join(n, _):
        here = pl.ds(pl.multiple_of(n * 64, 64), 64)
        state = came[here, :].astype(jnp.float32)
        cout[here, :] = (dec[here, :] * state + carry[here, :]).astype(jnp.bfloat16)
        carry[here, :] = state
        return 0

    def open_state(n, _):
        here = pl.ds(pl.multiple_of(n * 64, 64), 64)
        carry[here, :] = came[here, :].astype(jnp.float32)
        return 0

    def close_exact(n, _):
        here = pl.ds(pl.multiple_of(n * 64, 64), 64)
        rate = retain[here, :]
        last = carry[here, :]
        for s in range(1, span):
            last = (rate * factor[s]) * last + acc[s, here, :]
        cout[here, :] = last.astype(jnp.bfloat16)
        return 0

    share = side // CARRY_PIECES

    def carry_copy(q):
        here = pl.ds(q * share, share)
        return pltpu.make_async_remote_copy(
            src_ref=cout.at[here, :],
            dst_ref=came.at[here, :],
            send_sem=carry_send.at[q],
            recv_sem=carry_recv.at[q],
            device_id={"tm": lax.rem(j + 1, times)},
            device_id_type=MESH,
        )

    def inv_copy(s, d):
        return pltpu.make_async_remote_copy(
            src_ref=send2.at[s, d - 1],
            dst_ref=rowp.at[s, :, pl.ds(pl.multiple_of(z * cols, cols), cols)],
            send_sem=inv_send.at[s, d - 1],
            recv_sem=inv_recv.at[s, d - 1],
            device_id={"tile": partner(d)},
            device_id_type=MESH,
        )

    def inv_arrival(s, d):
        return pltpu.make_async_remote_copy(
            src_ref=send2.at[s, d - 1],
            dst_ref=rowp.at[s, :, pl.ds(pl.multiple_of(source(d) * cols, cols), cols)],
            send_sem=inv_send.at[s, d - 1],
            recv_sem=inv_recv.at[s, d - 1],
            device_id={"tile": partner(d)},
            device_id_type=MESH,
        )

    def inverse(s, _):
        fact = factor[s]

        def advance(n, _):
            here = pl.ds(pl.multiple_of(n * 128, 128), 128)
            now = (retain[here, :] * fact) * carry[here, :] + acc[s, here, :]
            carry[here, :] = now
            rb[here, :] = now.astype(jnp.bfloat16)
            return 0

        lax.fori_loop(0, side // 128, advance, 0)
        for d in list(range(1, tiles)) + [0]:
            mine = pl.ds(pl.multiple_of(partner(d) * rows, rows), rows)
            result = dot(bt[mine, :], rb[...]).astype(jnp.bfloat16)
            if d == 0:
                rowp[s, :, pl.ds(pl.multiple_of(z * cols, cols), cols)] = result
            else:
                send2[s, d - 1] = result
                inv_copy(s, d).start()
        return 0

    def quarter(q, body):
        lax.fori_loop(q * share // 64, (q + 1) * share // 64, body, 0)

    early = jnp.logical_and(lax.rem(j, 2) == 0, j > 0)
    last_first = runs == 1

    @pl.when(early)
    def _():
        first_frame = colp[runs - 1, 0]
        for m in range(side // 256):
            here = slice(m * 256, (m + 1) * 256)
            part = dot(bp[here, :], first_frame)
            acc[0, here, :] = part if last_first else acc[0, here, :] + part
        for q in range(CARRY_PIECES):
            carry_copy(q).wait_recv()
            quarter(q, open_state)

        inverse(0, 0)
        row_frames(runs - 1, last_first, 1)
        for q in range(CARRY_PIECES):
            quarter(q, close_exact)

            @pl.when(j < times - 1)
            def _(q=q):
                carry_copy(q).start()

        lax.fori_loop(1, span, inverse, 0)

    @pl.when(jnp.logical_not(early))
    def _():
        row_frames(runs - 1, last_first, 0)

        @pl.when(j == 0)
        def _():
            came[...] = jnp.zeros_like(came)

        for q in range(CARRY_PIECES):
            quarter(q, close)

            @pl.when(j > 0)
            def _(q=q):
                carry_copy(q).wait_recv()

            quarter(q, join)

            @pl.when(j < times - 1)
            def _(q=q):
                carry_copy(q).start()

        lax.fori_loop(0, span, inverse, 0)

    def finish(s, _):
        for d in range(1, tiles):
            inv_arrival(s, d).wait_recv()
        x[s] = lax.dot_general(
            rowp[s], bt[...], (((1,), (1,)), ((), ())), preferred_element_type=jnp.float32
        ).astype(jnp.bfloat16)
        pltpu.make_async_copy(x.at[s], out_hbm.at[s], out_sem.at[s]).start()
        return 0

    lax.fori_loop(0, span, finish, 0)

    def drain_frames(s, _):
        for d in range(1, tiles):
            inv_copy(s, d).wait_send()
        pltpu.make_async_copy(x.at[s], out_hbm.at[s], out_sem.at[s]).wait()
        return 0

    lax.fori_loop(0, span, drain_frames, 0)

    def drain_pieces(i, _):
        for d in range(1, tiles):
            fwd_copy(i, d).wait_send()
        for h in range(hops):

            @pl.when(sends(h))
            def _(h=h):
                hist_copy(h, i).wait_send()

        return 0

    lax.fori_loop(0, pieces, drain_pieces, 0)

    @pl.when(j < times - 1)
    def _():
        for q in range(CARRY_PIECES):
            carry_copy(q).wait_send()


def on_device(frames, inverse_taps, mode_rate, frame_factor):
    span, rows, side = frames.shape
    tap_count = inverse_taps.shape[0]
    tiles = side // rows
    cols = side // tiles
    pieces = rows // PIECE
    depth = tiles * PIECE * RUN
    hops = min((tap_count - 1 + span - 1) // span, lax.axis_size("tm") - 1)
    bt = jnp.asarray(cosine_table(side))
    any_space = pl.BlockSpec(memory_space=pl.ANY)
    smem = pl.BlockSpec(memory_space=pltpu.SMEM)
    b16, f32 = jnp.bfloat16, jnp.float32
    dma = pltpu.SemaphoreType.DMA
    return pl.pallas_call(
        kernel,
        out_shape=jax.ShapeDtypeStruct(frames.shape, b16),
        in_specs=[any_space, smem, any_space, smem, any_space],
        out_specs=any_space,
        scratch_shapes=[
            pltpu.VMEM((span, rows, side), b16),
            pltpu.VMEM((hops, span, rows, side), b16),
            pltpu.VMEM((side, side), b16),
            pltpu.VMEM((side, depth), b16),
            pltpu.VMEM((side, cols), f32),
            pltpu.VMEM((span, PIECE, side), b16),
            pltpu.VMEM((pieces, tiles - 1, span, PIECE, cols), b16),
            pltpu.VMEM((pieces // RUN, span, depth, cols), b16),
            pltpu.VMEM((span, side, cols), f32),
            pltpu.VMEM((span * GROUP, (hops + 1) * span * GROUP), f32),
            pltpu.VMEM((side, cols), f32),
            pltpu.VMEM((side, cols), b16),
            pltpu.VMEM((side, cols), b16),
            pltpu.VMEM((side, cols), f32),
            pltpu.VMEM((side, cols), b16),
            pltpu.VMEM((span, tiles - 1, rows, cols), b16),
            pltpu.VMEM((span, rows, side), b16),
            dma((3,)),
            dma((hops, pieces)),
            dma((hops, pieces)),
            dma((pieces, tiles - 1)),
            dma((pieces, tiles - 1)),
            dma((CARRY_PIECES,)),
            dma((CARRY_PIECES,)),
            dma((span, tiles - 1)),
            dma((span, tiles - 1)),
            dma((span,)),
        ],
        compiler_params=pltpu.CompilerParams(
            collective_id=0, has_side_effects=True, vmem_limit_bytes=67043328
        ),
    )(frames, inverse_taps, mode_rate, frame_factor, bt)


def solution(mesh):
    return jax.shard_map(
        on_device,
        mesh=mesh,
        in_specs=(P(("grp", "tm"), "tile", None), P(), P(None, "tile"), P(("grp", "tm"))),
        out_specs=P(("grp", "tm"), "tile", None),
        check_vma=False,
    )
```

```python
import jax
import jax.numpy as jnp
import numpy as np
from jax import lax
from jax.experimental import pallas as pl
from jax.experimental.pallas import tpu as pltpu
from jax.sharding import PartitionSpec as P

MESH = pl.DeviceIdType.MESH
GROUP = 16
PIECE = 16
RUN = 4
CARRY_PIECES = 4


def cosine_table(points):
    freq_idx = np.arange(points)[None, :]
    phase = (2 * np.arange(points)[:, None] + 1) * freq_idx % (4 * points)
    values = np.cos(np.pi * phase / (2.0 * points)) * np.sqrt(2.0 / points)
    values = np.where(freq_idx == 0, values / np.sqrt(2.0), values)
    return values.astype(np.float32).astype(jnp.bfloat16)


def dot(a, b):
    return jnp.dot(a, b, preferred_element_type=jnp.float32)


def kernel(
    x_hbm, taps, rate_hbm, factor, bt_hbm, out_hbm,
    x, hist, bt, bp, retain, flux, send1, colp, acc, tk, carry, came, cout, dec, rb, send2, rowp,
    load_sem, hist_send, hist_recv, fwd_send, fwd_recv, carry_send, carry_recv,
    inv_send, inv_recv, out_sem,
):
    span, rows, side = x.shape
    hops = hist.shape[0]
    runs, _, depth, cols = colp.shape
    pieces = runs * RUN
    tap_count = taps.shape[0]
    tiles = side // rows
    times = lax.axis_size("tm")
    j = lax.axis_index("tm")
    z = lax.axis_index("tile")

    def partner(d):
        return lax.rem(z + d, tiles)

    def source(d):
        return lax.rem(z + tiles - d, tiles)

    loads = [
        pltpu.make_async_copy(src, dst, load_sem.at[n])
        for n, (src, dst) in enumerate(((x_hbm, x), (bt_hbm, bt), (rate_hbm, retain)))
    ]
    for load in loads:
        load.start()

    barrier = pltpu.get_barrier_semaphore()
    for d in range(1, tiles):
        pl.semaphore_signal(barrier, inc=1, device_id={"tile": partner(d)}, device_id_type=MESH)

    for other in (lax.rem(j + 1, times), lax.rem(j + times - 1, times)):
        pl.semaphore_signal(barrier, inc=1, device_id={"tm": other}, device_id_type=MESH)

    pl.semaphore_wait(barrier, tiles + 1)

    def piece_rows(i):
        return pl.ds(pl.multiple_of(i * PIECE, PIECE), PIECE)

    def landing(i, owner):
        offset = lax.rem(i, RUN) * (depth // RUN) + owner * PIECE
        return colp.at[i // RUN, :, pl.ds(pl.multiple_of(offset, PIECE), PIECE), :]

    def hist_copy(h, i):
        src = x_hbm if h == 0 else hist.at[h - 1]
        return pltpu.make_async_remote_copy(
            src_ref=src.at[:, piece_rows(i), :],
            dst_ref=hist.at[h, :, piece_rows(i), :],
            send_sem=hist_send.at[h, i],
            recv_sem=hist_recv.at[h, i],
            device_id={"tm": lax.rem(j + 1, times)},
            device_id_type=MESH,
        )

    def sends(h):
        return jnp.logical_and(j < times - 1, j >= h)

    def fwd_copy(i, d):
        return pltpu.make_async_remote_copy(
            src_ref=send1.at[i, d - 1],
            dst_ref=landing(i, z),
            send_sem=fwd_send.at[i, d - 1],
            recv_sem=fwd_recv.at[i, d - 1],
            device_id={"tile": partner(d)},
            device_id_type=MESH,
        )

    def fwd_arrival(i, d):
        return pltpu.make_async_remote_copy(
            src_ref=send1.at[i, d - 1],
            dst_ref=landing(i, source(d)),
            send_sem=fwd_send.at[i, d - 1],
            recv_sem=fwd_recv.at[i, d - 1],
            device_id={"tile": partner(d)},
            device_id_type=MESH,
        )

    @pl.when(sends(0))
    def _():
        hist_copy(0, 0).start()

    wide = (hops + 1) * span * GROUP
    out_pos = lax.broadcasted_iota(jnp.int32, (span * GROUP, wide), 0)
    in_pos = lax.broadcasted_iota(jnp.int32, (span * GROUP, wide), 1)
    lag = out_pos // GROUP + hops * span - in_pos // GROUP
    lag = jnp.where(out_pos % GROUP == in_pos % GROUP, lag, -1)
    tk[...] = lag.astype(jnp.float32)

    def tap_rows(n, _):
        here = pl.ds(pl.multiple_of(n * GROUP, GROUP), GROUP)
        lags = tk[here, :]
        values = jnp.zeros_like(lags)
        for k in range(tap_count):
            values = jnp.where(lags == float(k), taps[k], values)
        tk[here, :] = values
        return 0

    lax.fori_loop(0, span, tap_rows, 0)

    loads[0].wait()
    loads[1].wait()

    def row_setup(n):
        pixels = [
            bt[pl.ds(pl.multiple_of(owner * rows + (n * RUN + part) * PIECE, PIECE), PIECE), :]
            for part in range(RUN)
            for owner in range(tiles)
        ]
        bp[...] = jnp.concatenate(pixels, axis=0).T
        for part in range(RUN):
            for d in range(1, tiles):
                fwd_arrival(n * RUN + part, d).wait_recv()

    def row_frames(n, first, start):
        def frame(s, _):
            block = colp[n, s]
            for m in range(side // 256):
                here = slice(m * 256, (m + 1) * 256)
                share = dot(bp[here, :], block)
                acc[s, here, :] = share if first else acc[s, here, :] + share
            return 0

        lax.fori_loop(start, span, frame, 0)

    def decay(n, _):
        here = pl.ds(pl.multiple_of(n * 64, 64), 64)
        retain[here, :] = jnp.exp(-retain[here, :])
        return 0

    def forward(i, _):
        for h in range(hops):

            @pl.when(j > h)
            def _(h=h):
                hist_copy(h, i).wait_recv()

            @pl.when(j <= h)
            def _(h=h):
                hist[h, :, piece_rows(i), :] = jnp.zeros((span, PIECE, side), hist.dtype)

            if h + 1 < hops:

                @pl.when(sends(h + 1))
                def _(h=h):
                    hist_copy(h + 1, i).start()

        @pl.when(jnp.logical_and(sends(0), i < pieces - 1))
        def _():
            hist_copy(0, i + 1).start()

        matrix = tk[...].astype(jnp.bfloat16)

        def group(n, _):
            here = pl.ds(pl.multiple_of(i * PIECE + n * GROUP, GROUP), GROUP)
            blocks = [hist[h, :, here, :].reshape(span * GROUP, side) for h in reversed(range(hops))]
            blocks.append(x[:, here, :].reshape(span * GROUP, side))
            result = dot(matrix, jnp.concatenate(blocks, axis=0)).astype(jnp.bfloat16)
            flux[:, pl.ds(pl.multiple_of(n * GROUP, GROUP), GROUP), :] = result.reshape(span, GROUP, side)
            return 0

        lax.fori_loop(0, PIECE // GROUP, group, 0)

        for d in list(range(1, tiles)) + [0]:
            modes = pl.ds(pl.multiple_of(partner(d) * cols, cols), cols)
            result = dot(flux[...].reshape(span * PIECE, side), bt[:, modes]).astype(jnp.bfloat16)
            result = result.reshape(span, PIECE, cols)
            if d == 0:
                landing(i, z)[...] = result
            else:
                send1[i, d - 1] = result
                fwd_copy(i, d).start()

        @pl.when(jnp.logical_and(lax.rem(i, RUN) == RUN - 1, i >= RUN))
        def _():
            n = i // RUN - 1
            row_setup(n)

            @pl.when(n == 0)
            def _():
                row_frames(n, True, 0)

            @pl.when(n > 0)
            def _():
                row_frames(n, False, 0)

        @pl.when(i == pieces - 1)
        def _():
            loads[2].wait()
            lax.fori_loop(0, side // 64, decay, 0)

        return 0

    lax.fori_loop(0, pieces, forward, 0)
    row_setup(runs - 1)

    def close(n, _):
        here = pl.ds(pl.multiple_of(n * 64, 64), 64)
        rate = retain[here, :]
        last = acc[0, here, :]
        whole = rate * factor[0]
        for s in range(1, span):
            now = rate * factor[s]
            last = now * last + acc[s, here, :]
            whole = now * whole
        carry[here, :] = last
        dec[here, :] = whole
        return 0

    def join(n, _):
        here = pl.ds(pl.multiple_of(n * 64, 64), 64)
        state = came[here, :].astype(jnp.float32)
        cout[here, :] = (dec[here, :] * state + carry[here, :]).astype(jnp.bfloat16)
        carry[here, :] = state
        return 0

    def open_state(n, _):
        here = pl.ds(pl.multiple_of(n * 64, 64), 64)
        carry[here, :] = came[here, :].astype(jnp.float32)
        return 0

    def close_exact(n, _):
        here = pl.ds(pl.multiple_of(n * 64, 64), 64)
        rate = retain[here, :]
        last = carry[here, :]
        for s in range(1, span):
            last = (rate * factor[s]) * last + acc[s, here, :]
        cout[here, :] = last.astype(jnp.bfloat16)
        return 0

    share = side // CARRY_PIECES

    def carry_copy(q):
        here = pl.ds(q * share, share)
        return pltpu.make_async_remote_copy(
            src_ref=cout.at[here, :],
            dst_ref=came.at[here, :],
            send_sem=carry_send.at[q],
            recv_sem=carry_recv.at[q],
            device_id={"tm": lax.rem(j + 1, times)},
            device_id_type=MESH,
        )

    def inv_copy(s, d):
        return pltpu.make_async_remote_copy(
            src_ref=send2.at[s, d - 1],
            dst_ref=rowp.at[s, :, pl.ds(pl.multiple_of(z * cols, cols), cols)],
            send_sem=inv_send.at[s, d - 1],
            recv_sem=inv_recv.at[s, d - 1],
            device_id={"tile": partner(d)},
            device_id_type=MESH,
        )

    def inv_arrival(s, d):
        return pltpu.make_async_remote_copy(
            src_ref=send2.at[s, d - 1],
            dst_ref=rowp.at[s, :, pl.ds(pl.multiple_of(source(d) * cols, cols), cols)],
            send_sem=inv_send.at[s, d - 1],
            recv_sem=inv_recv.at[s, d - 1],
            device_id={"tile": partner(d)},
            device_id_type=MESH,
        )

    def inverse(s, _):
        fact = factor[s]

        def advance(n, _):
            here = pl.ds(pl.multiple_of(n * 128, 128), 128)
            now = (retain[here, :] * fact) * carry[here, :] + acc[s, here, :]
            carry[here, :] = now
            rb[here, :] = now.astype(jnp.bfloat16)
            return 0

        lax.fori_loop(0, side // 128, advance, 0)
        for d in list(range(1, tiles)) + [0]:
            mine = pl.ds(pl.multiple_of(partner(d) * rows, rows), rows)
            result = dot(bt[mine, :], rb[...]).astype(jnp.bfloat16)
            if d == 0:
                rowp[s, :, pl.ds(pl.multiple_of(z * cols, cols), cols)] = result
            else:
                send2[s, d - 1] = result
                inv_copy(s, d).start()
        return 0

    def quarter(q, body):
        lax.fori_loop(q * share // 64, (q + 1) * share // 64, body, 0)

    early = jnp.logical_and(lax.rem(j, 2) == 0, j > 0)
    last_first = runs == 1

    @pl.when(early)
    def _():
        first_frame = colp[runs - 1, 0]
        for m in range(side // 256):
            here = slice(m * 256, (m + 1) * 256)
            part = dot(bp[here, :], first_frame)
            acc[0, here, :] = part if last_first else acc[0, here, :] + part
        for q in range(CARRY_PIECES):
            carry_copy(q).wait_recv()
            quarter(q, open_state)

        inverse(0, 0)
        row_frames(runs - 1, last_first, 1)
        for q in range(CARRY_PIECES):
            quarter(q, close_exact)

            @pl.when(j < times - 1)
            def _(q=q):
                carry_copy(q).start()

        lax.fori_loop(1, span, inverse, 0)

    @pl.when(jnp.logical_not(early))
    def _():
        row_frames(runs - 1, last_first, 0)

        @pl.when(j == 0)
        def _():
            came[...] = jnp.zeros_like(came)

        for q in range(CARRY_PIECES):
            quarter(q, close)

            @pl.when(j > 0)
            def _(q=q):
                carry_copy(q).wait_recv()

            quarter(q, join)

            @pl.when(j < times - 1)
            def _(q=q):
                carry_copy(q).start()

        lax.fori_loop(0, span, inverse, 0)

    def finish(s, _):
        for d in range(1, tiles):
            inv_arrival(s, d).wait_recv()
        x[s] = lax.dot_general(
            rowp[s], bt[...], (((1,), (1,)), ((), ())), preferred_element_type=jnp.float32
        ).astype(jnp.bfloat16)
        pltpu.make_async_copy(x.at[s], out_hbm.at[s], out_sem.at[s]).start()
        return 0

    lax.fori_loop(0, span, finish, 0)

    def drain_frames(s, _):
        for d in range(1, tiles):
            inv_copy(s, d).wait_send()
        pltpu.make_async_copy(x.at[s], out_hbm.at[s], out_sem.at[s]).wait()
        return 0

    lax.fori_loop(0, span, drain_frames, 0)

    def drain_pieces(i, _):
        for d in range(1, tiles):
            fwd_copy(i, d).wait_send()
        for h in range(hops):

            @pl.when(sends(h))
            def _(h=h):
                hist_copy(h, i).wait_send()

        return 0

    lax.fori_loop(0, pieces, drain_pieces, 0)

    @pl.when(j < times - 1)
    def _():
        for q in range(CARRY_PIECES):
            carry_copy(q).wait_send()


def on_device(frames, inverse_taps, mode_rate, frame_factor):
    span, rows, side = frames.shape
    tap_count = inverse_taps.shape[0]
    tiles = side // rows
    cols = side // tiles
    pieces = rows // PIECE
    depth = tiles * PIECE * RUN
    hops = min((tap_count - 1 + span - 1) // span, lax.axis_size("tm") - 1)
    bt = jnp.asarray(cosine_table(side))
    any_space = pl.BlockSpec(memory_space=pl.ANY)
    smem = pl.BlockSpec(memory_space=pltpu.SMEM)
    b16, f32 = jnp.bfloat16, jnp.float32
    dma = pltpu.SemaphoreType.DMA
    return pl.pallas_call(
        kernel,
        out_shape=jax.ShapeDtypeStruct(frames.shape, b16),
        in_specs=[any_space, smem, any_space, smem, any_space],
        out_specs=any_space,
        scratch_shapes=[
            pltpu.VMEM((span, rows, side), b16),
            pltpu.VMEM((hops, span, rows, side), b16),
            pltpu.VMEM((side, side), b16),
            pltpu.VMEM((side, depth), b16),
            pltpu.VMEM((side, cols), f32),
            pltpu.VMEM((span, PIECE, side), b16),
            pltpu.VMEM((pieces, tiles - 1, span, PIECE, cols), b16),
            pltpu.VMEM((pieces // RUN, span, depth, cols), b16),
            pltpu.VMEM((span, side, cols), f32),
            pltpu.VMEM((span * GROUP, (hops + 1) * span * GROUP), f32),
            pltpu.VMEM((side, cols), f32),
            pltpu.VMEM((side, cols), b16),
            pltpu.VMEM((side, cols), b16),
            pltpu.VMEM((side, cols), f32),
            pltpu.VMEM((side, cols), b16),
            pltpu.VMEM((span, tiles - 1, rows, cols), b16),
            pltpu.VMEM((span, rows, side), b16),
            dma((3,)),
            dma((hops, pieces)),
            dma((hops, pieces)),
            dma((pieces, tiles - 1)),
            dma((pieces, tiles - 1)),
            dma((CARRY_PIECES,)),
            dma((CARRY_PIECES,)),
            dma((span, tiles - 1)),
            dma((span, tiles - 1)),
            dma((span,)),
        ],
        compiler_params=pltpu.CompilerParams(
            collective_id=0, has_side_effects=True, vmem_limit_bytes=67043328
        ),
    )(frames, inverse_taps, mode_rate, frame_factor, bt)


def solution(mesh):
    return jax.shard_map(
        on_device,
        mesh=mesh,
        in_specs=(P(("grp", "tm"), "tile", None), P(), P(None, "tile"), P(("grp", "tm"))),
        out_specs=P(("grp", "tm"), "tile", None),
        check_vma=False,
    )
```

```python
import jax
import jax.numpy as jnp
import numpy as np
from jax import lax
from jax.experimental import pallas as pl
from jax.experimental.pallas import tpu as pltpu
from jax.sharding import PartitionSpec as P

MESH = pl.DeviceIdType.MESH
GROUP = 16
PIECE = 16
RUN = 4
CARRY_PIECES = 4


def cosine_table(points):
    freq_idx = np.arange(points)[None, :]
    phase = (2 * np.arange(points)[:, None] + 1) * freq_idx % (4 * points)
    values = np.cos(np.pi * phase / (2.0 * points)) * np.sqrt(2.0 / points)
    values = np.where(freq_idx == 0, values / np.sqrt(2.0), values)
    return values.astype(np.float32).astype(jnp.bfloat16)


def dot(a, b):
    return jnp.dot(a, b, preferred_element_type=jnp.float32)


def kernel(
    x_hbm, taps, rate_hbm, factor, bt_hbm, out_hbm,
    x, hist, bt, bp, retain, flux, send1, colp, acc, tk, carry, came, cout, dec, rb, send2, rowp,
    load_sem, hist_send, hist_recv, fwd_send, fwd_recv, carry_send, carry_recv,
    inv_send, inv_recv, out_sem,
):
    span, rows, side = x.shape
    hops = hist.shape[0]
    runs, _, depth, cols = colp.shape
    pieces = runs * RUN
    tap_count = taps.shape[0]
    tiles = side // rows
    times = lax.axis_size("tm")
    j = lax.axis_index("tm")
    z = lax.axis_index("tile")

    def partner(d):
        return lax.rem(z + d, tiles)

    def source(d):
        return lax.rem(z + tiles - d, tiles)

    loads = [
        pltpu.make_async_copy(src, dst, load_sem.at[n])
        for n, (src, dst) in enumerate(((x_hbm, x), (bt_hbm, bt), (rate_hbm, retain)))
    ]
    for load in loads:
        load.start()

    barrier = pltpu.get_barrier_semaphore()
    for d in range(1, tiles):
        pl.semaphore_signal(barrier, inc=1, device_id={"tile": partner(d)}, device_id_type=MESH)

    for other in (lax.rem(j + 1, times), lax.rem(j + times - 1, times)):
        pl.semaphore_signal(barrier, inc=1, device_id={"tm": other}, device_id_type=MESH)

    pl.semaphore_wait(barrier, tiles + 1)

    def piece_rows(i):
        return pl.ds(pl.multiple_of(i * PIECE, PIECE), PIECE)

    def landing(i, owner):
        offset = lax.rem(i, RUN) * (depth // RUN) + owner * PIECE
        return colp.at[i // RUN, :, pl.ds(pl.multiple_of(offset, PIECE), PIECE), :]

    def hist_copy(h, i):
        src = x_hbm if h == 0 else hist.at[h - 1]
        return pltpu.make_async_remote_copy(
            src_ref=src.at[:, piece_rows(i), :],
            dst_ref=hist.at[h, :, piece_rows(i), :],
            send_sem=hist_send.at[h, i],
            recv_sem=hist_recv.at[h, i],
            device_id={"tm": lax.rem(j + 1, times)},
            device_id_type=MESH,
        )

    def sends(h):
        return jnp.logical_and(j < times - 1, j >= h)

    def fwd_copy(i, d):
        return pltpu.make_async_remote_copy(
            src_ref=send1.at[i, d - 1],
            dst_ref=landing(i, z),
            send_sem=fwd_send.at[i, d - 1],
            recv_sem=fwd_recv.at[i, d - 1],
            device_id={"tile": partner(d)},
            device_id_type=MESH,
        )

    def fwd_arrival(i, d):
        return pltpu.make_async_remote_copy(
            src_ref=send1.at[i, d - 1],
            dst_ref=landing(i, source(d)),
            send_sem=fwd_send.at[i, d - 1],
            recv_sem=fwd_recv.at[i, d - 1],
            device_id={"tile": partner(d)},
            device_id_type=MESH,
        )

    @pl.when(sends(0))
    def _():
        hist_copy(0, 0).start()

    wide = (hops + 1) * span * GROUP
    out_pos = lax.broadcasted_iota(jnp.int32, (span * GROUP, wide), 0)
    in_pos = lax.broadcasted_iota(jnp.int32, (span * GROUP, wide), 1)
    lag = out_pos // GROUP + hops * span - in_pos // GROUP
    lag = jnp.where(out_pos % GROUP == in_pos % GROUP, lag, -1)
    tk[...] = lag.astype(jnp.float32)

    def tap_rows(n, _):
        here = pl.ds(pl.multiple_of(n * GROUP, GROUP), GROUP)
        lags = tk[here, :]
        values = jnp.zeros_like(lags)
        for k in range(tap_count):
            values = jnp.where(lags == float(k), taps[k], values)
        tk[here, :] = values
        return 0

    lax.fori_loop(0, span, tap_rows, 0)

    loads[0].wait()
    loads[1].wait()

    def row_setup(n):
        pixels = [
            bt[pl.ds(pl.multiple_of(owner * rows + (n * RUN + part) * PIECE, PIECE), PIECE), :]
            for part in range(RUN)
            for owner in range(tiles)
        ]
        bp[...] = jnp.concatenate(pixels, axis=0).T
        for part in range(RUN):
            for d in range(1, tiles):
                fwd_arrival(n * RUN + part, d).wait_recv()

    def row_frames(n, first, start):
        def frame(s, _):
            block = colp[n, s]
            for m in range(side // 256):
                here = slice(m * 256, (m + 1) * 256)
                share = dot(bp[here, :], block)
                acc[s, here, :] = share if first else acc[s, here, :] + share
            return 0

        lax.fori_loop(start, span, frame, 0)

    def decay(n, _):
        here = pl.ds(pl.multiple_of(n * 64, 64), 64)
        retain[here, :] = jnp.exp(-retain[here, :])
        return 0

    def forward(i, _):
        for h in range(hops):

            @pl.when(j > h)
            def _(h=h):
                hist_copy(h, i).wait_recv()

            @pl.when(j <= h)
            def _(h=h):
                hist[h, :, piece_rows(i), :] = jnp.zeros((span, PIECE, side), hist.dtype)

            if h + 1 < hops:

                @pl.when(sends(h + 1))
                def _(h=h):
                    hist_copy(h + 1, i).start()

        @pl.when(jnp.logical_and(sends(0), i < pieces - 1))
        def _():
            hist_copy(0, i + 1).start()

        matrix = tk[...].astype(jnp.bfloat16)

        def group(n, _):
            here = pl.ds(pl.multiple_of(i * PIECE + n * GROUP, GROUP), GROUP)
            blocks = [hist[h, :, here, :].reshape(span * GROUP, side) for h in reversed(range(hops))]
            blocks.append(x[:, here, :].reshape(span * GROUP, side))
            result = dot(matrix, jnp.concatenate(blocks, axis=0)).astype(jnp.bfloat16)
            flux[:, pl.ds(pl.multiple_of(n * GROUP, GROUP), GROUP), :] = result.reshape(span, GROUP, side)
            return 0

        lax.fori_loop(0, PIECE // GROUP, group, 0)

        for d in sorted(range(1, tiles), key=lambda d: abs(2 * d - tiles)) + [0]:
            modes = pl.ds(pl.multiple_of(partner(d) * cols, cols), cols)
            result = dot(flux[...].reshape(span * PIECE, side), bt[:, modes]).astype(jnp.bfloat16)
            result = result.reshape(span, PIECE, cols)
            if d == 0:
                landing(i, z)[...] = result
            else:
                send1[i, d - 1] = result
                fwd_copy(i, d).start()

        @pl.when(jnp.logical_and(lax.rem(i, RUN) == RUN - 1, i >= RUN))
        def _():
            n = i // RUN - 1
            row_setup(n)

            @pl.when(n == 0)
            def _():
                row_frames(n, True, 0)

            @pl.when(n > 0)
            def _():
                row_frames(n, False, 0)

        @pl.when(i == pieces - 1)
        def _():
            loads[2].wait()
            lax.fori_loop(0, side // 64, decay, 0)

        return 0

    lax.fori_loop(0, pieces, forward, 0)
    row_setup(runs - 1)

    def close(n, _):
        here = pl.ds(pl.multiple_of(n * 64, 64), 64)
        rate = retain[here, :]
        last = acc[0, here, :]
        whole = rate * factor[0]
        for s in range(1, span):
            now = rate * factor[s]
            last = now * last + acc[s, here, :]
            whole = now * whole
        carry[here, :] = last
        dec[here, :] = whole
        return 0

    def join(n, _):
        here = pl.ds(pl.multiple_of(n * 64, 64), 64)
        state = came[here, :].astype(jnp.float32)
        cout[here, :] = (dec[here, :] * state + carry[here, :]).astype(jnp.bfloat16)
        carry[here, :] = state
        return 0

    def open_state(n, _):
        here = pl.ds(pl.multiple_of(n * 64, 64), 64)
        carry[here, :] = came[here, :].astype(jnp.float32)
        return 0

    def close_exact(n, _):
        here = pl.ds(pl.multiple_of(n * 64, 64), 64)
        rate = retain[here, :]
        last = carry[here, :]
        for s in range(1, span):
            last = (rate * factor[s]) * last + acc[s, here, :]
        cout[here, :] = last.astype(jnp.bfloat16)
        return 0

    share = side // CARRY_PIECES

    def carry_copy(q):
        here = pl.ds(q * share, share)
        return pltpu.make_async_remote_copy(
            src_ref=cout.at[here, :],
            dst_ref=came.at[here, :],
            send_sem=carry_send.at[q],
            recv_sem=carry_recv.at[q],
            device_id={"tm": lax.rem(j + 1, times)},
            device_id_type=MESH,
        )

    def inv_copy(s, d):
        return pltpu.make_async_remote_copy(
            src_ref=send2.at[s, d - 1],
            dst_ref=rowp.at[s, :, pl.ds(pl.multiple_of(z * cols, cols), cols)],
            send_sem=inv_send.at[s, d - 1],
            recv_sem=inv_recv.at[s, d - 1],
            device_id={"tile": partner(d)},
            device_id_type=MESH,
        )

    def inv_arrival(s, d):
        return pltpu.make_async_remote_copy(
            src_ref=send2.at[s, d - 1],
            dst_ref=rowp.at[s, :, pl.ds(pl.multiple_of(source(d) * cols, cols), cols)],
            send_sem=inv_send.at[s, d - 1],
            recv_sem=inv_recv.at[s, d - 1],
            device_id={"tile": partner(d)},
            device_id_type=MESH,
        )

    def inverse(s, _):
        fact = factor[s]

        def advance(n, _):
            here = pl.ds(pl.multiple_of(n * 128, 128), 128)
            now = (retain[here, :] * fact) * carry[here, :] + acc[s, here, :]
            carry[here, :] = now
            rb[here, :] = now.astype(jnp.bfloat16)
            return 0

        lax.fori_loop(0, side // 128, advance, 0)
        for d in sorted(range(1, tiles), key=lambda d: abs(2 * d - tiles)) + [0]:
            mine = pl.ds(pl.multiple_of(partner(d) * rows, rows), rows)
            result = dot(bt[mine, :], rb[...]).astype(jnp.bfloat16)
            if d == 0:
                rowp[s, :, pl.ds(pl.multiple_of(z * cols, cols), cols)] = result
            else:
                send2[s, d - 1] = result
                inv_copy(s, d).start()
        return 0

    def quarter(q, body):
        lax.fori_loop(q * share // 64, (q + 1) * share // 64, body, 0)

    early = jnp.logical_and(lax.rem(j, 2) == 0, j > 0)
    last_first = runs == 1

    @pl.when(early)
    def _():
        first_frame = colp[runs - 1, 0]
        for m in range(side // 256):
            here = slice(m * 256, (m + 1) * 256)
            part = dot(bp[here, :], first_frame)
            acc[0, here, :] = part if last_first else acc[0, here, :] + part
        for q in range(CARRY_PIECES):
            carry_copy(q).wait_recv()
            quarter(q, open_state)

        inverse(0, 0)
        row_frames(runs - 1, last_first, 1)
        for q in range(CARRY_PIECES):
            quarter(q, close_exact)

            @pl.when(j < times - 1)
            def _(q=q):
                carry_copy(q).start()

        lax.fori_loop(1, span, inverse, 0)

    @pl.when(jnp.logical_not(early))
    def _():
        row_frames(runs - 1, last_first, 0)

        @pl.when(j == 0)
        def _():
            came[...] = jnp.zeros_like(came)

        for q in range(CARRY_PIECES):
            quarter(q, close)

            @pl.when(j > 0)
            def _(q=q):
                carry_copy(q).wait_recv()

            quarter(q, join)

            @pl.when(j < times - 1)
            def _(q=q):
                carry_copy(q).start()

        lax.fori_loop(0, span, inverse, 0)

    def finish(s, _):
        for d in range(1, tiles):
            inv_arrival(s, d).wait_recv()
        x[s] = lax.dot_general(
            rowp[s], bt[...], (((1,), (1,)), ((), ())), preferred_element_type=jnp.float32
        ).astype(jnp.bfloat16)
        pltpu.make_async_copy(x.at[s], out_hbm.at[s], out_sem.at[s]).start()
        return 0

    lax.fori_loop(0, span, finish, 0)

    def drain_frames(s, _):
        for d in range(1, tiles):
            inv_copy(s, d).wait_send()
        pltpu.make_async_copy(x.at[s], out_hbm.at[s], out_sem.at[s]).wait()
        return 0

    lax.fori_loop(0, span, drain_frames, 0)

    def drain_pieces(i, _):
        for d in range(1, tiles):
            fwd_copy(i, d).wait_send()
        for h in range(hops):

            @pl.when(sends(h))
            def _(h=h):
                hist_copy(h, i).wait_send()

        return 0

    lax.fori_loop(0, pieces, drain_pieces, 0)

    @pl.when(j < times - 1)
    def _():
        for q in range(CARRY_PIECES):
            carry_copy(q).wait_send()


def on_device(frames, inverse_taps, mode_rate, frame_factor):
    span, rows, side = frames.shape
    tap_count = inverse_taps.shape[0]
    tiles = side // rows
    cols = side // tiles
    pieces = rows // PIECE
    depth = tiles * PIECE * RUN
    hops = min((tap_count - 1 + span - 1) // span, lax.axis_size("tm") - 1)
    bt = jnp.asarray(cosine_table(side))
    any_space = pl.BlockSpec(memory_space=pl.ANY)
    smem = pl.BlockSpec(memory_space=pltpu.SMEM)
    b16, f32 = jnp.bfloat16, jnp.float32
    dma = pltpu.SemaphoreType.DMA
    return pl.pallas_call(
        kernel,
        out_shape=jax.ShapeDtypeStruct(frames.shape, b16),
        in_specs=[any_space, smem, any_space, smem, any_space],
        out_specs=any_space,
        scratch_shapes=[
            pltpu.VMEM((span, rows, side), b16),
            pltpu.VMEM((hops, span, rows, side), b16),
            pltpu.VMEM((side, side), b16),
            pltpu.VMEM((side, depth), b16),
            pltpu.VMEM((side, cols), f32),
            pltpu.VMEM((span, PIECE, side), b16),
            pltpu.VMEM((pieces, tiles - 1, span, PIECE, cols), b16),
            pltpu.VMEM((pieces // RUN, span, depth, cols), b16),
            pltpu.VMEM((span, side, cols), f32),
            pltpu.VMEM((span * GROUP, (hops + 1) * span * GROUP), f32),
            pltpu.VMEM((side, cols), f32),
            pltpu.VMEM((side, cols), b16),
            pltpu.VMEM((side, cols), b16),
            pltpu.VMEM((side, cols), f32),
            pltpu.VMEM((side, cols), b16),
            pltpu.VMEM((span, tiles - 1, rows, cols), b16),
            pltpu.VMEM((span, rows, side), b16),
            dma((3,)),
            dma((hops, pieces)),
            dma((hops, pieces)),
            dma((pieces, tiles - 1)),
            dma((pieces, tiles - 1)),
            dma((CARRY_PIECES,)),
            dma((CARRY_PIECES,)),
            dma((span, tiles - 1)),
            dma((span, tiles - 1)),
            dma((span,)),
        ],
        compiler_params=pltpu.CompilerParams(
            collective_id=0, has_side_effects=True, vmem_limit_bytes=67043328
        ),
    )(frames, inverse_taps, mode_rate, frame_factor, bt)


def solution(mesh):
    return jax.shard_map(
        on_device,
        mesh=mesh,
        in_specs=(P(("grp", "tm"), "tile", None), P(), P(None, "tile"), P(("grp", "tm"))),
        out_specs=P(("grp", "tm"), "tile", None),
        check_vma=False,
    )
```
